32 devices in a mesh: dp: 4 (over y, x), expert: 8 (over z, core).
Axes of the slice: x: 2, y: 2, z: 4, core: 2. Of those that a mesh axis runs over, the one named last changes fastest.
Arguments:
- tokens: bfloat16 [1024, 7168], P('expert', 'dp'), may hold values from -6 to 6
- gate_scores: float32 [1024, 8], P('expert'), may hold values from 0.05 to 0.45
- expert_ids: int32 [1024, 8], P('expert'), may hold values from 0 to 15, all different within a row; in each aligned block of 128 rows (0 to 127, 128 to 255, ...) at most 96 rows name the same one
- matching: int32 [8], replicated, may hold values from 0 to 7, as said below
- w_in: bfloat16 [16, 2, 7168, 2048], P('expert', None, 'dp'), may hold values from -0.0625 to 0.0625
- w_out: bfloat16 [16, 2048, 7168], P('expert', None, 'dp'), may hold values from -0.125 to 0.125
Outputs:
- mixed: bfloat16 [1024, 7168], P('expert', 'dp')
- moved_in: bfloat16 [16, 2, 7168, 2048], P('expert', None, 'dp')
- moved_out: bfloat16 [16, 2048, 7168], P('expert', None, 'dp')
The draws below stay inside these ranges and needn't reach their ends.
Inputs may be any that keep to these rules, and one draw needn't show every extreme that they name: The pairing is symmetric: entry j is j itself or the index 4 away, and matching[matching[j]] = j. Entry 7 is always 8/2 - 1. `expert_ids`: each row names 8 different experts. Within the 128 rows of one device (aligned blocks) no expert is named more than 96 times, a bound that some block reaches.
All inputs are finite; a program needn't handle non-finite values.
Results may differ from the reference program's by a relative error of at most 0.019.
Values may be sent and summed in bfloat16 or wider, within the bound.
No kernel may reach another device: no remote copies, remote signals or barrier semaphores. Data moves between devices by JAX's collectives and lax.ppermute only.
A program may use at most 256 MiB of HBM per device.

```python
import math
import jax
import jax.numpy as jnp
import numpy as np
from jax import lax

D = 7168
FF = 2048
TOP = 8
EXPERTS = 16
TOK_DEV = 128
OWNERS = 8
EXP_DEV = 2
CAP = 96
TOKENS = 1024
N_DP = 4


def draw_matching(key, part):
    count = EXPERTS // EXP_DEV
    half = count // 2
    flags = jax.random.randint(key, (half,), 0, 2, dtype=jnp.int32)
    flags = flags.at[half - 1].set(1)
    lower = jnp.arange(half, dtype=jnp.int32)
    first = lower + half * flags
    second = lower + half * (1 - flags)
    return jnp.concatenate([first, second]).astype(jnp.int32)


def level_of(stream_key, shape, cuts, low, largest):
    factor_of, own = 1.0, jax.random.fold_in(stream_key, 6)
    for dim, shards_of in cuts:
        heights = jnp.exp(jax.random.uniform(jax.random.fold_in(own, dim), (shards_of,), jnp.float32, low / len(cuts), largest / len(cuts)))
        factor_of = factor_of * jnp.repeat(heights, shape[dim] // shards_of).reshape([-1 if axis == dim else 1 for axis in range(len(shape))])
    return factor_of


def assign_block(own_key, own, number, rows, number_of, top, reach, skew):
    order = jax.random.permutation(own_key, number_of)
    crowded, common = portions_of(number_of, rows * top, reach, skew, True), portions_of(number_of, rows * top, reach, skew, False)
    places = jnp.arange(number_of)

    def named(sizes, turn):
        used = int((sizes > 0).sum())
        fixed = max(1, used // 4)
        moved = fixed + (places - fixed + turn * (used - fixed)) % max(1, number_of - fixed)
        return jnp.zeros((number_of,), jnp.int32).at[order[jnp.where(places < fixed, places, moved)]].set(jnp.asarray(sizes, jnp.int32))

    sizes = jnp.where(number % 4 == 0, named(crowded, number // 4), named(common, number - number // 4 - 1))
    mixed = jax.random.permutation(jax.random.fold_in(own, 3), number_of)
    donor, receiver = mixed[0:number_of // 2 * 2:2], mixed[1:number_of // 2 * 2:2]
    margin = jnp.minimum(sizes[donor] - 1, reach - sizes[receiver]) // 2
    margin = jnp.where((donor == order[0]) | (receiver == order[0]) | (sizes[receiver] == 0), 0, jnp.maximum(margin, 0))
    moved = jax.random.randint(jax.random.fold_in(own, 4), (number_of // 2,), 0, 1 << 20) % (margin + 1)
    sizes = sizes.at[donor].add(-moved).at[receiver].add(moved)
    items = jnp.searchsorted(jnp.cumsum(sizes), jnp.arange(rows * top), side="right").astype(jnp.int32)
    listing = items.reshape(top, rows).T
    listing = listing[jax.random.permutation(jax.random.fold_in(own, 1), rows)]
    turn = jax.random.randint(jax.random.fold_in(own, 2), (rows, 1), 0, top)
    return jnp.take_along_axis(listing, (jnp.arange(top)[None, :] + turn) % top, axis=1)


def portions_of(amount, total, reach, skew, full):
    portions = [(1 << 20) // math.isqrt(grade ** skew) + 1 for grade in range(1, amount + 1)]
    largest = reach if full else min(reach, max(-(-total // amount), total * portions[0] // sum(portions)))
    least = 1 if total - largest >= amount - 1 else 0
    holding, rest = [largest] + [least] * (amount - 1), total - largest - least * (amount - 1)
    while rest > 0:
        movable = [i for i in range(1, amount) if holding[i] < largest] or [i for i in range(1, amount) if holding[i] < reach]
        mass, remaining = sum([portions[i] for i in movable]), rest
        for i in movable:
            extra = min(reach - holding[i], max(1, remaining * portions[i] // mass), rest)
            holding[i] = holding[i] + extra
            rest = rest - extra
    return np.array(holding)


def normal_values(rng, extent, scale, reach, shards=(), kind=jnp.bfloat16):
    level = level_of(rng, extent, shards, -0.22, 0.18) if shards else 1.0
    drawn = jax.random.normal(rng, extent, jnp.float32) * scale * level
    return jnp.minimum(jnp.maximum(drawn, -reach), reach).astype(kind)


def setup_inputs(seed: int = 0) -> dict:
    keys = jax.random.split(jax.random.key(seed), 7)
    tokens = normal_values(keys[0], (TOKENS, D), 1.0, 6.0, ((0, 8), (1, 4)))
    gate_scores = jnp.clip(0.05 + 0.39999999 * jax.random.uniform(keys[1], (TOKENS, TOP), jnp.float32) ** level_of(keys[1], (TOKENS, TOP), ((0, 8),), -0.2, 0.2), 0.05, 0.45)
    expert_ids_keys = jax.random.split(jax.random.fold_in(keys[2], 1), TOKENS // TOK_DEV)
    expert_ids_turns = jax.random.permutation(jax.random.fold_in(keys[2], 3), TOKENS // TOK_DEV)
    expert_ids = jax.vmap(lambda own, number: assign_block(jax.random.fold_in(keys[2], 2), own, number, TOK_DEV, EXPERTS, TOP, CAP, 2))(expert_ids_keys, expert_ids_turns).reshape((TOKENS, TOP))
    matching = draw_matching(jax.random.fold_in(keys[6], 71), 0)
    w_in = normal_values(keys[4], (EXPERTS, 2, D, FF), D ** -0.5, 0.0625, ((0, 8), (2, 4)))
    w_out = normal_values(keys[5], (EXPERTS, FF, D), FF ** -0.5, 0.125, ((0, 8), (2, 4)))
    return dict(tokens=tokens, gate_scores=gate_scores, expert_ids=expert_ids, matching=matching, w_in=w_in, w_out=w_out)


def reference(tokens, gate_scores, expert_ids, matching, w_in, w_out):
    local = jnp.arange(EXP_DEV, dtype=jnp.int32)
    source = (matching[:, None] * EXP_DEV + local[None, :]).reshape(-1).astype(jnp.int32)
    moved_in = w_in[source]
    moved_out = w_out[source]
    flat_ids = expert_ids.reshape(-1).astype(jnp.int32)
    labels = jnp.arange(EXPERTS, dtype=jnp.int32)
    onehot = (flat_ids[:, None] == labels[None, :]).astype(jnp.int32)
    ranks = jnp.cumsum(onehot, axis=0) - 1
    slot = jnp.sum(ranks * onehot, axis=1).astype(jnp.int32)
    rows_max = OWNERS * CAP
    token_of = (jnp.arange(TOKENS * TOP, dtype=jnp.int32) // TOP).astype(jnp.int32)
    block_width = D // N_DP

    def one_expert(expert):
        position = jnp.where(flat_ids == expert, slot, rows_max).astype(jnp.int32)
        index = jnp.zeros((rows_max,), jnp.int32).at[position].set(token_of, mode="drop")
        buffer = tokens[index]
        weights = w_in[expert]
        gate = jnp.zeros((rows_max, FF), jnp.float32)
        upper = jnp.zeros((rows_max, FF), jnp.float32)
        for block in range(N_DP):
            lo_col = block * block_width
            rows_part = buffer[:, lo_col:lo_col + block_width]
            gate_part = jnp.dot(rows_part, weights[0, lo_col:lo_col + block_width], preferred_element_type=jnp.float32)
            upper_part = jnp.dot(rows_part, weights[1, lo_col:lo_col + block_width], preferred_element_type=jnp.float32)
            gate = gate + gate_part.astype(jnp.bfloat16).astype(jnp.float32)
            upper = upper + upper_part.astype(jnp.bfloat16).astype(jnp.float32)
        hidden = (jax.nn.silu(gate) * upper).astype(jnp.bfloat16)
        return jnp.dot(hidden, w_out[expert], preferred_element_type=jnp.float32).astype(jnp.bfloat16)

    outputs = lax.map(one_expert, labels)
    picked = outputs[flat_ids, slot].astype(jnp.float32).reshape(TOKENS, TOP, D)
    mixed = jnp.sum(picked * gate_scores[:, :, None], axis=1).astype(jnp.bfloat16)
    return (mixed, moved_in, moved_out)
```

```python
import jax
import jax.numpy as jnp
from jax import lax
from jax.sharding import PartitionSpec as P

GROUPS = 4
LANES = 128
CUTS = (0, 8, 12, 14, 15, 16)


def pair_groups(owners):
    half = owners // 2
    count = min(GROUPS, half)
    size = half // count
    return [range(g * size, (g + 1) * size) for g in range(count)]


def exchange(route, staying, w_in, w_out):
    got_in = lax.ppermute(w_in, "expert", route)
    rows = w_out.shape[0] * w_out.shape[1]
    flat = w_out.reshape(rows, w_out.shape[2])
    moved_out = flat
    edges = [rows * c // CUTS[-1] for c in CUTS]
    for low, high in zip(edges[:-1], edges[1:]):
        own = flat[low:high]
        got = lax.ppermute(own, "expert", route)
        piece = jnp.where(staying, own, got)
        moved_out = lax.dynamic_update_slice(moved_out, piece, (low, 0))
    moved_in = jnp.where(staying, w_in, got_in)
    return moved_in, moved_out.reshape(w_out.shape)


def routed(tokens, gate_scores, expert_ids, w_in, w_out):
    owners = lax.axis_size("expert")
    here = lax.axis_index("expert")
    parts = lax.axis_size("dp")
    exp_dev, halves, features, hidden_units = w_in.shape
    experts = owners * exp_dev
    rows = tokens.shape[0] * owners
    labels = jnp.arange(experts, dtype=jnp.int32)
    named = expert_ids[:, :, None] == labels
    weight = jnp.sum(jnp.where(named, gate_scores[:, :, None], 0.0), axis=1)
    digits, rest = [], weight
    for _ in range(3):
        digit = lax.reduce_precision(rest, 8, 7)
        digits.append(digit.astype(jnp.bfloat16))
        rest = rest - digit
    pad = jnp.zeros((tokens.shape[0], -3 * experts % LANES), jnp.bfloat16)
    sent = jnp.concatenate([tokens, *digits, pad], axis=1)
    everything = lax.all_gather(sent, "expert", axis=0, tiled=True)
    all_tokens = everything[:, :features]
    quarter = rows // parts
    first = lax.axis_index("dp") * quarter
    mine = 0.0
    for d in range(3):
        start = features + d * experts + here * exp_dev
        digit = lax.dynamic_slice(everything, (first, start), (quarter, exp_dev))
        mine = mine + digit.astype(jnp.float32)
    total = None
    for l in range(exp_dev):
        summed = []
        for g in range(halves):
            partial = jnp.dot(all_tokens, w_in[l, g], preferred_element_type=jnp.float32)
            partial = partial.astype(jnp.bfloat16)
            partial = lax.psum_scatter(partial, "dp", scatter_dimension=0, tiled=True)
            summed.append(partial.astype(jnp.float32))
        gate, up = summed
        hidden = (jax.nn.silu(gate) * up * mine[:, l : l + 1]).astype(jnp.bfloat16)
        hidden = lax.all_gather(hidden, "dp", axis=0, tiled=True)
        result = jnp.dot(hidden, w_out[l], preferred_element_type=jnp.float32)
        total = result if total is None else total + result
    return lax.psum_scatter(
        total.astype(jnp.bfloat16), "expert", scatter_dimension=0, tiled=True
    )


def shards(tokens, gate_scores, expert_ids, matching, w_in, w_out):
    owners = lax.axis_size("expert")
    half = owners // 2
    here = lax.axis_index("expert")
    staying = matching[here] == here
    groups = pair_groups(owners)

    def branch(pattern):
        route = []
        for g, members in enumerate(groups):
            if g == len(groups) - 1 or pattern >> g & 1:
                for j in members:
                    route += [(j, j + half), (j + half, j)]

        def run(tokens, gate_scores, expert_ids, staying, w_in, w_out):
            moved_in, moved_out = exchange(route, staying, w_in, w_out)
            mixed = routed(tokens, gate_scores, expert_ids, w_in, w_out)
            return mixed, moved_in, moved_out

        return run

    pattern = jnp.int32(0)
    for g, members in enumerate(groups[:-1]):
        swaps = matching[members.start : members.stop] != jnp.arange(members.start, members.stop)
        pattern = pattern | jnp.any(swaps).astype(jnp.int32) << g
    branches = [branch(p) for p in range(1 << (len(groups) - 1))]
    return lax.switch(
        pattern, branches, tokens, gate_scores, expert_ids, staying, w_in, w_out
    )


def solution(mesh):
    in_specs = (
        P("expert", "dp"),
        P("expert", None),
        P("expert", None),
        P(),
        P("expert", None, "dp", None),
        P("expert", None, "dp"),
    )
    out_specs = (P("expert", "dp"), P("expert", None, "dp", None), P("expert", None, "dp"))
    return jax.shard_map(shards, mesh=mesh, in_specs=in_specs, out_specs=out_specs, check_vma=False)
```

```python
import functools

import jax
import jax.numpy as jnp
from jax import lax
from jax.sharding import Mesh
from jax.sharding import PartitionSpec as P

GROUPS = 4
LANES = 128
OWNER = ("chip", "core")


def pair_groups(owners):
    half = owners // 2
    count = min(GROUPS, half)
    size = half // count
    return [range(g * size, (g + 1) * size) for g in range(count)]


def both_ways(members, half):
    return [pair for j in members for pair in ((j, j + half), (j + half, j))]


def chosen(staying, early, own, first, got):
    return jnp.where(staying, own, jnp.where(early, first, got))


def exchange(route, staying, early, w_in, w_out, early_in):
    if not route:
        moved_in = jnp.where(staying, w_in, early_in)
        return lax.optimization_barrier((moved_in, jnp.zeros_like(w_out)))
    got_in = lax.ppermute(w_in, OWNER, route)
    got_out = lax.ppermute(w_out, OWNER, route)
    moved_in = chosen(staying, early, w_in, early_in, got_in)
    return lax.optimization_barrier((moved_in, got_out))


def gathered(tokens, gate_scores, expert_ids, experts):
    labels = jnp.arange(experts, dtype=jnp.int32)
    named = expert_ids[:, :, None] == labels
    weight = jnp.sum(jnp.where(named, gate_scores[:, :, None], 0.0), axis=1)
    digits, rest = [], weight
    for _ in range(3):
        digit = lax.reduce_precision(rest, 8, 7)
        digits.append(digit.astype(jnp.bfloat16))
        rest = rest - digit
    pad = jnp.zeros((tokens.shape[0], -3 * experts % LANES), jnp.bfloat16)
    sent = jnp.concatenate([tokens, *digits, pad], axis=1)
    lane = lax.all_gather(sent, "chip", axis=0, tiled=True)
    return lax.all_gather(lane, "core", axis=0, tiled=True)


def routed(everything, w_in, w_out):
    here = lax.axis_index(OWNER)
    parts = lax.axis_size("dp")
    exp_dev, halves, features, hidden_units = w_in.shape
    experts = lax.axis_size(OWNER) * exp_dev
    rows = everything.shape[0]
    all_tokens = everything[:, :features]
    quarter = rows // parts
    first = lax.axis_index("dp") * quarter
    mine = 0.0
    for d in range(3):
        start = features + d * experts + here * exp_dev
        digit = lax.dynamic_slice(everything, (first, start), (quarter, exp_dev))
        mine = mine + digit.astype(jnp.float32)
    total = None
    for l in range(exp_dev):
        summed = []
        for g in range(halves):
            partial = jnp.dot(all_tokens, w_in[l, g], preferred_element_type=jnp.float32)
            partial = partial.astype(jnp.bfloat16)
            partial = lax.psum_scatter(partial, "dp", scatter_dimension=0, tiled=True)
            summed.append(partial.astype(jnp.float32))
        gate, up = summed
        hidden = (jax.nn.silu(gate) * up * mine[:, l : l + 1]).astype(jnp.bfloat16)
        hidden = lax.all_gather(hidden, "dp", axis=0, tiled=True)
        result = jnp.dot(hidden, w_out[l], preferred_element_type=jnp.float32)
        total = result if total is None else total + result
    return total.astype(jnp.bfloat16)


def blank(everything, w_in, w_out):
    return jnp.zeros((everything.shape[0], w_out.shape[2]), jnp.bfloat16)


def returned(total):
    lane = lax.psum_scatter(total, "core", scatter_dimension=0, tiled=True)
    return lax.psum_scatter(lane, "chip", scatter_dimension=0, tiled=True)


def shards(tokens, gate_scores, expert_ids, matching, w_in, w_out):
    owners = lax.axis_size(OWNER)
    half = owners // 2
    here = lax.axis_index(OWNER)
    staying = matching[here] == here
    whole = matching[owners - 1] == half - 1
    groups = pair_groups(owners)

    early = jnp.any(here % half == jnp.arange(groups[-1].start, groups[-1].stop))
    first = both_ways(groups[-1], half)
    early_in = lax.ppermute(w_in, OWNER, first)
    early_out = lax.ppermute(w_out, OWNER, first)
    everything = gathered(tokens, gate_scores, expert_ids, owners * w_in.shape[0])
    total = lax.cond(whole, routed, blank, everything, w_in, w_out)
    mixed = returned(total)
    early_in, early_out, total = lax.optimization_barrier((early_in, early_out, total))
    pattern = jnp.int32(0)
    for g, members in enumerate(groups[:-1]):
        swaps = matching[members.start : members.stop] != jnp.arange(members.start, members.stop)
        pattern = pattern | jnp.any(swaps).astype(jnp.int32) << g
    branches = []
    for p in range(1 << (len(groups) - 1)):
        active = [j for g, members in enumerate(groups[:-1]) if p >> g & 1 for j in members]
        branches.append(functools.partial(exchange, both_ways(active, half)))
    w_out, early_in, early_out = lax.optimization_barrier((w_out, early_in, early_out))
    moved_in, got_out = lax.switch(pattern, branches, staying, early, w_in, w_out, early_in)
    moved_out = chosen(staying, early, w_out, early_out, got_out)
    return mixed, moved_in, moved_out


def solution(mesh):
    cores = mesh.devices.reshape(mesh.shape["dp"], mesh.shape["expert"] // 2, 2)
    inner = Mesh(cores, ("dp", "chip", "core"))
    in_specs = (
        P(OWNER, "dp"),
        P(OWNER, None),
        P(OWNER, None),
        P(),
        P(OWNER, None, "dp", None),
        P(OWNER, None, "dp"),
    )
    out_specs = (P(OWNER, "dp"), P(OWNER, None, "dp", None), P(OWNER, None, "dp"))
    return jax.shard_map(shards, mesh=inner, in_specs=in_specs, out_specs=out_specs, check_vma=False)
```

```python
import functools

import jax
import jax.numpy as jnp
from jax import lax
from jax.sharding import Mesh
from jax.sharding import PartitionSpec as P

GROUPS = 4
LANES = 128
OWNER = ("chip", "core")


def pair_groups(owners):
    half = owners // 2
    count = min(GROUPS, half)
    size = half // count
    return [range(g * size, (g + 1) * size) for g in range(count)]


def both_ways(members, half):
    return [pair for j in members for pair in ((j, j + half), (j + half, j))]


def chosen(staying, early, own, first, got):
    return jnp.where(staying, own, jnp.where(early, first, got))


def exchange(route, staying, early, w_in, w_out, early_in):
    if not route:
        moved_in = jnp.where(staying, w_in, early_in)
        return lax.optimization_barrier((moved_in, jnp.zeros_like(w_out)))
    got_in = lax.ppermute(w_in, OWNER, route)
    got_out = lax.ppermute(w_out, OWNER, route)
    moved_in = chosen(staying, early, w_in, early_in, got_in)
    return lax.optimization_barrier((moved_in, got_out))


def gathered(tokens, gate_scores, expert_ids, experts):
    labels = jnp.arange(experts, dtype=jnp.int32)
    named = expert_ids[:, :, None] == labels
    weight = jnp.sum(jnp.where(named, gate_scores[:, :, None], 0.0), axis=1)
    digits, rest = [], weight
    for _ in range(3):
        digit = lax.reduce_precision(rest, 8, 7)
        digits.append(digit.astype(jnp.bfloat16))
        rest = rest - digit
    pad = jnp.zeros((tokens.shape[0], -3 * experts % LANES), jnp.bfloat16)
    sent = jnp.concatenate([tokens, *digits, pad], axis=1)
    lane = lax.all_gather(sent, "chip", axis=0, tiled=True)
    return lax.all_gather(lane, "core", axis=0, tiled=True)


def routed(everything, w_in, w_out):
    here = lax.axis_index(OWNER)
    parts = lax.axis_size("dp")
    exp_dev, halves, features, hidden_units = w_in.shape
    experts = lax.axis_size(OWNER) * exp_dev
    rows = everything.shape[0]
    all_tokens = everything[:, :features]
    quarter = rows // parts
    first = lax.axis_index("dp") * quarter
    mine = 0.0
    for d in range(3):
        start = features + d * experts + here * exp_dev
        digit = lax.dynamic_slice(everything, (first, start), (quarter, exp_dev))
        mine = mine + digit.astype(jnp.float32)
    total = None
    for l in range(exp_dev):
        summed = []
        for g in range(halves):
            partial = jnp.dot(all_tokens, w_in[l, g], preferred_element_type=jnp.float32)
            partial = partial.astype(jnp.bfloat16)
            partial = lax.psum_scatter(partial, "dp", scatter_dimension=0, tiled=True)
            summed.append(partial.astype(jnp.float32))
        gate, up = summed
        hidden = (jax.nn.silu(gate) * up * mine[:, l : l + 1]).astype(jnp.bfloat16)
        hidden = lax.all_gather(hidden, "dp", axis=0, tiled=True)
        result = jnp.dot(hidden, w_out[l], preferred_element_type=jnp.float32)
        total = result if total is None else total + result
    return total.astype(jnp.bfloat16)


def blank(everything, w_in, w_out):
    return jnp.zeros((everything.shape[0], w_out.shape[2]), jnp.bfloat16)


def returned(total):
    lane = lax.psum_scatter(total, "core", scatter_dimension=0, tiled=True)
    return lax.psum_scatter(lane, "chip", scatter_dimension=0, tiled=True)


def shards(tokens, gate_scores, expert_ids, matching, w_in, w_out):
    owners = lax.axis_size(OWNER)
    half = owners // 2
    here = lax.axis_index(OWNER)
    staying = matching[here] == here
    whole = matching[owners - 1] == half - 1
    groups = pair_groups(owners)

    early = jnp.any(here % half == jnp.arange(groups[-1].start, groups[-1].stop))
    first = both_ways(groups[-1], half)
    early_in = lax.ppermute(w_in, OWNER, first)
    early_out = lax.ppermute(w_out, OWNER, first)
    everything = gathered(tokens, gate_scores, expert_ids, owners * w_in.shape[0])
    total = lax.cond(whole, routed, blank, everything, w_in, w_out)
    mixed = returned(total)
    early_in, total = lax.optimization_barrier((early_in, total))
    pattern = jnp.int32(0)
    for g, members in enumerate(groups[:-1]):
        swaps = matching[members.start : members.stop] != jnp.arange(members.start, members.stop)
        pattern = pattern | jnp.any(swaps).astype(jnp.int32) << g
    branches = []
    for p in range(1 << (len(groups) - 1)):
        active = [j for g, members in enumerate(groups[:-1]) if p >> g & 1 for j in members]
        branches.append(functools.partial(exchange, both_ways(active, half)))
    moved_in, got_out = lax.switch(pattern, branches, staying, early, w_in, w_out, early_in)
    moved_out = chosen(staying, early, w_out, early_out, got_out)
    return mixed, moved_in, moved_out


def solution(mesh):
    cores = mesh.devices.reshape(mesh.shape["dp"], mesh.shape["expert"] // 2, 2)
    inner = Mesh(cores, ("dp", "chip", "core"))
    in_specs = (
        P(OWNER, "dp"),
        P(OWNER, None),
        P(OWNER, None),
        P(),
        P(OWNER, None, "dp", None),
        P(OWNER, None, "dp"),
    )
    out_specs = (P(OWNER, "dp"), P(OWNER, None, "dp", None), P(OWNER, None, "dp"))
    return jax.shard_map(shards, mesh=inner, in_specs=in_specs, out_specs=out_specs, check_vma=False)
```
